32 devices in a mesh: case: 2 (over y), panel: 4 (over z), slab: 2 (over x), obs: 2 (over core).
Axes of the slice: x: 2, y: 2, z: 4, core: 2. Of those that a mesh axis runs over, the one named last changes fastest.
Arguments:
- loading: bfloat16 [65536, 512], P(('case', 'panel'), 'slab'), parts along dimension 0, may hold values from -6 to 6
- green: bfloat16 [128, 32768], P(('case', 'obs'), 'panel'), parts along dimension 0, may hold values from -0.03125 to 0.03125
- delays: int32 [128, 2048], P(('case', 'obs'), 'panel'), parts along dimension 0, may hold values from 0 to 120
- offsets: int32 [128, 2048], P(('case', 'obs'), 'panel'), parts along dimension 0, may hold values from 0 to 7
- live_groups: int32 [8], P('case'), parts along dimension 0, may hold values from 1 to 4, as said below
Outputs:
- signal: float32 [128, 512], P(('case', 'obs'), 'slab'), parts along dimension 0
The draws below stay inside these ranges and needn't reach their ends.
There are 2 independent parts, one for each index of `case`. The reference program is written for one: setup_inputs(seed, part) draws one part's arguments, and reference() takes and returns one part's arrays. A program takes and returns all parts, laid end to end along the dimension named above; each array names one. Nothing has to cross between parts.
Inputs may be any that keep to these rules, and one draw needn't show every extreme that they name: `live_groups`: in every draw some sector has all 4 groups live while the sector 4/2 positions away has one.
All inputs are finite; a program needn't handle non-finite values.
Results may differ from the reference program's by a relative error of at most 0.0034.
Values may be sent and summed in bfloat16 or wider, within the bound.
A program may use at most 64 MiB of HBM per device.

```python
import jax
import jax.numpy as jnp
from jax import lax

OBS = 64
BP = 16
GB = 128
GROUPS = 4
LAGS = 128
SECTORS = 4
PANELS = 32768
BLOCKS = 2048
TSAMP = 512


def draw_live_groups(key, part):
    first_key, second_key, third_key = jax.random.split(jax.random.fold_in(key, 17), 3)
    heavy = jax.random.randint(first_key, (SECTORS,), 0, 3) == 0
    extra = jax.random.randint(second_key, (SECTORS,), 2, GROUPS + 1)
    counts = jnp.where(heavy, extra, 1).astype(jnp.int32)
    picked = jax.random.randint(third_key, (), 0, SECTORS)
    counts = counts.at[picked].set(GROUPS)
    partner = jnp.bitwise_xor(picked, SECTORS // 2)
    counts = counts.at[partner].set(1)
    return counts.astype(jnp.int32)


def touch_ends(entries, stream_key, least, high):
    longest = entries.shape.index(max(entries.shape))
    spots = []
    for shift in (0, 1):
        where = [jax.random.randint(jax.random.fold_in(stream_key, axis), (), 0, length) for axis, length in enumerate(entries.shape)]
        where[longest] = (where[longest] + shift) % entries.shape[longest]
        spots.append(tuple(where))
    return entries.at[spots[0]].set(least).at[spots[1]].set(high)


def level_of(stream_key, shape, shards, smallest, largest):
    factor_of, own = 1.0, jax.random.fold_in(stream_key, 6)
    for axis_at, blocks in shards:
        steps = jnp.exp(jax.random.uniform(jax.random.fold_in(own, axis_at), (blocks,), jnp.float32, smallest / len(shards), largest / len(shards)))
        factor_of = factor_of * jnp.repeat(steps, shape[axis_at] // blocks).reshape([-1 if axis == axis_at else 1 for axis in range(len(shape))])
    return factor_of


def normal_values(key, shape, spread, reach, pieces=(), kind=jnp.bfloat16):
    level = level_of(key, shape, pieces, -0.22, 0.18) if pieces else 1.0
    values = jax.random.normal(key, shape, jnp.float32) * spread * level
    return jnp.minimum(jnp.maximum(values, -reach), reach).astype(kind)


def setup_inputs(seed: int = 0, part: int = 0) -> dict:
    arg_keys = jax.random.split(jax.random.key(seed), 6)
    own_keys = jax.random.split(jax.random.fold_in(arg_keys[5], part), 6)
    loading = normal_values(own_keys[0], (PANELS, TSAMP), 1.0, 6.0, ((0, 4), (1, 2)))
    green = normal_values(own_keys[1], (OBS, PANELS), PANELS ** -0.5, 0.03125, ((0, 2), (1, 4)))
    delays = touch_ends(jax.random.randint(own_keys[2], (OBS, BLOCKS), 0, LAGS - 7), jax.random.fold_in(own_keys[2], 1), 0, (LAGS - 7) - 1).astype(jnp.int32)
    offsets = touch_ends(jax.random.randint(own_keys[3], (OBS, BLOCKS), 0, 8), jax.random.fold_in(own_keys[3], 1), 0, 7).astype(jnp.int32)
    live_groups = draw_live_groups(jax.random.fold_in(jax.random.fold_in(arg_keys[5], part), 71), part)
    return dict(loading=loading, green=green, delays=delays, offsets=offsets, live_groups=live_groups)


def lagrange_weights(offset_part):
    position = 3.0 + offset_part.astype(jnp.float32) / 8.0
    weights = []
    for tap in range(8):
        factor = jnp.ones_like(position)
        for other in range(8):
            if other != tap:
                factor = factor * (position - other) / (tap - other)
        weights.append(factor)
    return weights


def build_table(delay_part, offset_part, lag_count):
    lag_index = jnp.arange(lag_count, dtype=jnp.int32)[None, :, None]
    relative = lag_index - delay_part.astype(jnp.int32)[:, None, :]
    weights = lagrange_weights(offset_part)
    table_sum = jnp.zeros(relative.shape, jnp.float32)
    for tap in range(8):
        table_sum = table_sum + jnp.where(relative == tap, weights[tap][:, None, :], 0.0)
    return table_sum.astype(jnp.bfloat16)


def reference(loading, green, delays, offsets, live_groups):
    samples = loading.shape[1]
    group_count = SECTORS * GROUPS
    grouped_load = loading.reshape(group_count, GB, BP, samples)
    grouped_green = jnp.moveaxis(green.reshape(OBS, group_count, GB, BP), 1, 0)
    grouped_delay = jnp.moveaxis(delays.reshape(OBS, group_count, GB), 1, 0)
    grouped_offset = jnp.moveaxis(offsets.reshape(OBS, group_count, GB), 1, 0)
    fft_length = samples + LAGS

    def compute(group_index):
        block_signal = jnp.einsum("obp,bpt->bot", grouped_green[group_index].astype(jnp.float32),
                                  grouped_load[group_index].astype(jnp.float32)).astype(jnp.bfloat16)
        block_signal = lax.optimization_barrier(block_signal).astype(jnp.float32)
        lag_table = build_table(grouped_delay[group_index], grouped_offset[group_index], LAGS)
        lag_table = lax.optimization_barrier(lag_table).astype(jnp.float32)
        signal_spectrum = jnp.fft.rfft(block_signal, fft_length, axis=2)
        table_spectrum = jnp.fft.rfft(jnp.transpose(lag_table, (2, 0, 1)), fft_length, axis=2)
        combined = jnp.sum(signal_spectrum * table_spectrum, axis=0)
        return jnp.fft.irfft(combined, fft_length, axis=1)[:, :samples].astype(jnp.float32)

    def skipped(group_index):
        return jnp.zeros((OBS, samples), jnp.float32)

    def step_group(carried, group_index):
        sector = group_index // GROUPS
        is_live = live_groups[sector] > group_index % GROUPS
        return carried + lax.cond(is_live, compute, skipped, group_index), None

    start_sum = jnp.zeros((OBS, samples), jnp.float32)
    signal, unused = lax.scan(step_group, start_sum, jnp.arange(group_count, dtype=jnp.int32))
    return signal
```

```python
import functools
import math

import jax
import jax.numpy as jnp
from jax import lax
from jax.experimental import pallas as pl
from jax.experimental.pallas import tpu as pltpu
from jax.sharding import PartitionSpec as P

BP = 16
GB = 128
LAGS = 128
TAPS = 8
KT = 256
LANES = 128
ROWS = 8
LOAD_CHUNKS = 8
UNROLL = 2
MESH = pl.DeviceIdType.MESH


def kernel(panels, slabs, live_ref, load_hbm, green_hbm, delay_hbm, offset_hbm, out_ref,
           load_ref, green_in, green_f32, delay_ref, offset_ref, weight_ref, block_ref, part_ref,
           main_in, tail_in, load_sem, small_sem, main_send, main_recv, tail_send, tail_recv):
    panel = lax.axis_index("panel")
    slab = lax.axis_index("slab")
    n_panels, samples = load_hbm.shape
    observers = green_hbm.shape[0]
    blocks = delay_hbm.shape[1]
    chunks = observers // ROWS
    tiles = n_panels // KT
    per_load = n_panels // LOAD_CHUNKS
    has_next = slab < slabs - 1
    has_prev = slab > 0

    smalls = [pltpu.make_async_copy(src, dst, small_sem.at[i]) for i, (src, dst) in enumerate(
        ((green_hbm, green_in), (delay_hbm, delay_ref), (offset_hbm, offset_ref)))]
    for copy in smalls:
        copy.start()
    loads = []
    for c in range(LOAD_CHUNKS):
        rows = pl.ds(c * per_load, per_load)
        loads.append(pltpu.make_async_copy(load_hbm.at[rows, :], load_ref.at[rows, :], load_sem.at[c]))
        loads[-1].start()

    barrier = pltpu.get_barrier_semaphore()
    for d in range(1, panels):
        pl.semaphore_signal(barrier, inc=1, device_id={"panel": lax.rem(panel + d, panels)}, device_id_type=MESH)

    @pl.when(has_next)
    def _():
        for d in range(panels):
            pl.semaphore_signal(barrier, inc=1, device_id={
                "panel": lax.rem(panel + d, panels), "slab": slab + 1}, device_id_type=MESH)

    @pl.when(has_prev)
    def _():
        for d in range(panels):
            pl.semaphore_signal(barrier, inc=1, device_id={
                "panel": lax.rem(panel + d, panels), "slab": slab - 1}, device_id_type=MESH)

    for copy in smalls[1:]:
        copy.wait()
    position = 3.0 + offset_ref[...].astype(jnp.float32) * 0.125
    terms = [position - float(m) for m in range(TAPS)]
    before = [None] * TAPS
    after = [None] * TAPS
    for k in range(1, TAPS):
        before[k] = terms[k - 1] if k == 1 else before[k - 1] * terms[k - 1]
    for k in range(TAPS - 2, -1, -1):
        after[k] = terms[k + 1] if k == TAPS - 2 else after[k + 1] * terms[k + 1]
    for k in range(TAPS):
        scale = 1.0 / math.prod(k - m for m in range(TAPS) if m != k)
        if k == 0:
            value = after[k]
        elif k == TAPS - 1:
            value = before[k]
        else:
            value = before[k] * after[k]
        weight_ref[k] = value * scale
    live = live_ref[panel]
    group_of = lax.broadcasted_iota(jnp.int32, (observers, blocks), 1) // GB
    delay_ref[...] = jnp.where(group_of < live, delay_ref[...], 4 * LAGS)

    smalls[0].wait()
    green_f32[...] = green_in[...].astype(jnp.float32)
    block_row = lax.broadcasted_iota(jnp.int32, (BP, KT), 0)
    panel_col = lax.broadcasted_iota(jnp.int32, (BP, KT), 1)
    diagonal = jnp.where(panel_col // BP == block_row, 1.0, 0.0).astype(jnp.bfloat16)

    def tile_step(tile, carry):
        columns = pl.ds(pl.multiple_of(tile * KT, KT), KT)
        pieces = []
        for o in range(observers):
            row = jnp.broadcast_to(green_f32[o:o + 1, columns], (BP, KT)).astype(jnp.bfloat16)
            pieces.append(row * diagonal)
        spread = jnp.concatenate(pieces, axis=0)
        product = jnp.dot(spread, load_ref[columns, :], preferred_element_type=jnp.float32)
        block_ref[:, pl.ds(pl.multiple_of(tile * BP, BP), BP), :] = (
            product.astype(jnp.bfloat16).reshape(observers, BP, samples))
        return carry

    tiles_per_load = tiles // LOAD_CHUNKS
    for c in range(LOAD_CHUNKS):
        loads[c].wait()
        lax.fori_loop(c * tiles_per_load, (c + 1) * tiles_per_load, tile_step, 0)

    sub = lax.broadcasted_iota(jnp.int32, (BP, blocks), 0)
    lane = lax.broadcasted_iota(jnp.int32, (8, LANES), 1)
    row8 = lax.broadcasted_iota(jnp.int32, (8, LANES), 0)
    wide = samples // LANES
    zero = jnp.zeros((8, LANES), jnp.float32)

    def shifted_in(parts, keep):
        return [jnp.where(keep, parts[0], 0.0)] + [
            jnp.where(keep, parts[j], parts[j - 1]) for j in range(1, len(parts))]

    def observer_step(o, carry):
        behind = sub - delay_ref[pl.ds(o, 1), :]
        tap = behind & (BP - 1)
        place = ((BP - 1 - behind) >> 4).astype(jnp.float32).astype(jnp.bfloat16)
        stencil = jnp.zeros((BP, blocks), jnp.float32)
        for k in range(TAPS):
            stencil = jnp.where(tap == k, weight_ref[k, pl.ds(o, 1), :], stencil)
        stencil = stencil.astype(jnp.bfloat16)
        table = jnp.concatenate([
            jnp.where(place == jnp.bfloat16(q), stencil, jnp.bfloat16(0)) for q in range(LAGS // BP)], axis=0)
        lagged = jnp.dot(table, block_ref[o], preferred_element_type=jnp.float32)
        sums = [zero] * (wide + 1)
        for high in range(LAGS // 8):
            shift = 8 * high
            parts = [lagged[shift:shift + 8, j * LANES:(j + 1) * LANES] for j in range(wide)]
            if shift == 0:
                moved = parts + [None]
            else:
                parts = [pltpu.roll(part, shift, 1) for part in parts]
                keep = lane >= shift
                moved = shifted_in(parts, keep) + [jnp.where(keep, 0.0, parts[-1])]
            sums = [a if b is None else a + b for a, b in zip(sums, moved)]
        sums = [pltpu.roll(part, 0, 1, stride=1, stride_axis=0) for part in sums]
        sums = shifted_in(sums, lane >= row8)
        own = row8 == lax.rem(o, ROWS)
        return tuple(
            jnp.where(own, jnp.sum(part, axis=0, keepdims=True), kept) for part, kept in zip(sums, carry))

    def main_copy(c, d):
        return pltpu.make_async_remote_copy(
            src_ref=part_ref.at[pl.ds(c * ROWS, ROWS), pl.ds(0, samples)],
            dst_ref=main_in.at[c, d - 1],
            send_sem=main_send.at[c, d - 1], recv_sem=main_recv.at[c, d - 1],
            device_id={"panel": lax.rem(panel + d, panels)}, device_id_type=MESH)

    def tail_copy(c, d):
        return pltpu.make_async_remote_copy(
            src_ref=part_ref.at[pl.ds(c * ROWS, ROWS), pl.ds(samples, LAGS)],
            dst_ref=tail_in.at[c, d],
            send_sem=tail_send.at[c, d], recv_sem=tail_recv.at[c, d],
            device_id={"panel": lax.rem(panel + d, panels), "slab": slab + 1}, device_id_type=MESH)

    for c in range(chunks):
        gathered = lax.fori_loop(
            c * ROWS, (c + 1) * ROWS, observer_step, (zero,) * (wide + 1), unroll=UNROLL)
        for j in range(wide + 1):
            part_ref[c * ROWS:(c + 1) * ROWS, j * LANES:(j + 1) * LANES] = gathered[j]
        if c == 0:
            pl.semaphore_wait(barrier, panels - 1 + panels * (has_next.astype(jnp.int32) + has_prev.astype(jnp.int32)))

        for d in range(1, panels):
            main_copy(c, d).start()

        @pl.when(has_next)
        def _():
            for d in range(panels):
                tail_copy(c, d).start()

    for c in range(chunks):
        rows = slice(c * ROWS, (c + 1) * ROWS)
        total = part_ref[rows, :samples]
        for d in range(1, panels):
            main_copy(c, d).wait_recv()
            total = total + main_in[c, d - 1]
        out_ref[rows, :] = total

        @pl.when(has_prev)
        def _():
            late = None
            for d in range(panels):
                tail_copy(c, d).wait_recv()
                late = tail_in[c, d] if late is None else late + tail_in[c, d]
            out_ref[rows, :LAGS] += late

    for c in range(chunks):
        for d in range(1, panels):
            main_copy(c, d).wait_send()

        @pl.when(has_next)
        def _():
            for d in range(panels):
                tail_copy(c, d).wait_send()


def shards(panels, slabs, loading, green, delays, offsets, live_groups):
    n_panels, samples = loading.shape
    observers = green.shape[0]
    blocks = delays.shape[1]
    chunks = observers // ROWS
    peers = max(panels - 1, 1)
    anywhere = pl.BlockSpec(memory_space=pl.ANY)
    return pl.pallas_call(
        functools.partial(kernel, panels, slabs),
        out_shape=jax.ShapeDtypeStruct((observers, samples), jnp.float32),
        in_specs=[pl.BlockSpec(memory_space=pltpu.SMEM)] + [anywhere] * 4,
        out_specs=pl.BlockSpec(memory_space=pltpu.VMEM),
        scratch_shapes=[
            pltpu.VMEM((n_panels, samples), jnp.bfloat16),
            pltpu.VMEM((observers, n_panels), jnp.bfloat16),
            pltpu.VMEM((observers, n_panels), jnp.float32),
            pltpu.VMEM((observers, blocks), jnp.int32),
            pltpu.VMEM((observers, blocks), jnp.int32),
            pltpu.VMEM((TAPS, observers, blocks), jnp.float32),
            pltpu.VMEM((observers, blocks, samples), jnp.bfloat16),
            pltpu.VMEM((observers, samples + LAGS), jnp.float32),
            pltpu.VMEM((chunks, peers, ROWS, samples), jnp.float32),
            pltpu.VMEM((chunks, panels, ROWS, LAGS), jnp.float32),
            pltpu.SemaphoreType.DMA((LOAD_CHUNKS,)),
            pltpu.SemaphoreType.DMA((3,)),
            pltpu.SemaphoreType.DMA((chunks, peers)),
            pltpu.SemaphoreType.DMA((chunks, peers)),
            pltpu.SemaphoreType.DMA((chunks, panels)),
            pltpu.SemaphoreType.DMA((chunks, panels)),
        ],
        compiler_params=pltpu.CompilerParams(
            collective_id=0, has_side_effects=True, vmem_limit_bytes=56 * 2 ** 20),
        name="far_field",
    )(live_groups, loading, green, delays, offsets)


def solution(mesh):
    placed = (
        P(("case", "panel"), "slab"),
        P(("case", "obs"), "panel"),
        P(("case", "obs"), "panel"),
        P(("case", "obs"), "panel"),
        P("case"),
    )
    return jax.shard_map(
        functools.partial(shards, mesh.shape["panel"], mesh.shape["slab"]),
        mesh=mesh, in_specs=placed, out_specs=P(("case", "obs"), "slab"), check_vma=False,
    )
```

```python
import functools
import math

import jax
import jax.numpy as jnp
from jax import lax
from jax.experimental import pallas as pl
from jax.experimental.pallas import tpu as pltpu
from jax.sharding import PartitionSpec as P

BP = 16
GB = 128
LAGS = 128
TAPS = 8
KT = 256
LANES = 128
ROWS = 8
LOAD_CHUNKS = 8
UNROLL = 8
MESH = pl.DeviceIdType.MESH


def kernel(panels, slabs, live_ref, load_hbm, green_hbm, delay_hbm, offset_hbm, out_ref,
           load_ref, green_in, green_f32, delay_ref, offset_ref, weight_ref, block_ref, part_ref,
           main_out, tail_out, main_in, tail_in, load_sem, green_sem, small_sem, main_send, main_recv, tail_send, tail_recv):
    panel = lax.axis_index("panel")
    slab = lax.axis_index("slab")
    n_panels, samples = load_hbm.shape
    observers = green_hbm.shape[0]
    blocks = delay_hbm.shape[1]
    chunks = observers // ROWS
    tiles = n_panels // KT
    per_load = n_panels // LOAD_CHUNKS
    has_next = slab < slabs - 1
    has_prev = slab > 0

    smalls = [pltpu.make_async_copy(src, dst, small_sem.at[i]) for i, (src, dst) in enumerate(
        ((delay_hbm, delay_ref), (offset_hbm, offset_ref)))]
    loads, greens = [], []
    for c in range(LOAD_CHUNKS):
        rows = pl.ds(c * per_load, per_load)
        greens.append(pltpu.make_async_copy(green_hbm.at[:, rows], green_in.at[:, rows], green_sem.at[c]))
        greens[-1].start()
        loads.append(pltpu.make_async_copy(load_hbm.at[rows, :], load_ref.at[rows, :], load_sem.at[c]))
        loads[-1].start()
    for copy in smalls:
        copy.start()

    barrier = pltpu.get_barrier_semaphore()
    for d in range(1, panels):
        pl.semaphore_signal(barrier, inc=1, device_id={"panel": lax.rem(panel + d, panels)}, device_id_type=MESH)

    @pl.when(has_next)
    def _():
        for d in range(panels):
            pl.semaphore_signal(barrier, inc=1, device_id={
                "panel": lax.rem(panel + d, panels), "slab": slab + 1}, device_id_type=MESH)

    @pl.when(has_prev)
    def _():
        for d in range(panels):
            pl.semaphore_signal(barrier, inc=1, device_id={
                "panel": lax.rem(panel + d, panels), "slab": slab - 1}, device_id_type=MESH)

    block_row = lax.broadcasted_iota(jnp.int32, (BP, KT), 0)
    panel_col = lax.broadcasted_iota(jnp.int32, (BP, KT), 1)
    diagonal = jnp.where(panel_col // BP == block_row, 1.0, 0.0).astype(jnp.bfloat16)

    def tile_step(tile, carry):
        columns = pl.ds(pl.multiple_of(tile * KT, KT), KT)
        pieces = []
        for o in range(observers):
            row = jnp.broadcast_to(green_f32[o:o + 1, columns], (BP, KT)).astype(jnp.bfloat16)
            pieces.append(row * diagonal)
        spread = jnp.concatenate(pieces, axis=0)
        product = jnp.dot(spread, load_ref[columns, :], preferred_element_type=jnp.float32)
        block_ref[:, pl.ds(pl.multiple_of(tile * BP, BP), BP), :] = (
            product.astype(jnp.bfloat16).reshape(observers, BP, samples))
        return carry

    tiles_per_load = tiles // LOAD_CHUNKS
    for c in range(LOAD_CHUNKS):
        greens[c].wait()
        columns = slice(c * per_load, (c + 1) * per_load)
        green_f32[:, columns] = green_in[:, columns].astype(jnp.float32)
        loads[c].wait()
        lax.fori_loop(c * tiles_per_load, (c + 1) * tiles_per_load, tile_step, 0, unroll=4)

    for copy in smalls:
        copy.wait()
    position = 3.0 + offset_ref[...].astype(jnp.float32) * 0.125
    terms = [position - float(m) for m in range(TAPS)]
    before = [None] * TAPS
    after = [None] * TAPS
    for k in range(1, TAPS):
        before[k] = terms[k - 1] if k == 1 else before[k - 1] * terms[k - 1]
    for k in range(TAPS - 2, -1, -1):
        after[k] = terms[k + 1] if k == TAPS - 2 else after[k + 1] * terms[k + 1]
    for k in range(TAPS):
        scale = 1.0 / math.prod(k - m for m in range(TAPS) if m != k)
        if k == 0:
            value = after[k]
        elif k == TAPS - 1:
            value = before[k]
        else:
            value = before[k] * after[k]
        weight_ref[k] = value * scale
    live = live_ref[panel]
    group_of = lax.broadcasted_iota(jnp.int32, (observers, blocks), 1) // GB
    delay_ref[...] = jnp.where(group_of < live, delay_ref[...], 4 * LAGS)

    sub = lax.broadcasted_iota(jnp.int32, (BP, blocks), 0)
    lane = lax.broadcasted_iota(jnp.int32, (8, LANES), 1)
    row8 = lax.broadcasted_iota(jnp.int32, (8, LANES), 0)
    wide = samples // LANES
    zero = jnp.zeros((8, LANES), jnp.float32)

    def shifted_in(parts, keep):
        return [jnp.where(keep, parts[0], 0.0)] + [
            jnp.where(keep, parts[j], parts[j - 1]) for j in range(1, len(parts))]

    def observer_step(o, carry):
        behind = sub - delay_ref[pl.ds(o, 1), :]
        tap = behind & (BP - 1)
        place = ((BP - 1 - behind) >> 4).astype(jnp.float32).astype(jnp.bfloat16)
        stencil = jnp.zeros((BP, blocks), jnp.float32)
        for k in range(TAPS):
            stencil = jnp.where(tap == k, weight_ref[k, pl.ds(o, 1), :], stencil)
        stencil = stencil.astype(jnp.bfloat16)
        table = jnp.concatenate([
            jnp.where(place == jnp.bfloat16(q), stencil, jnp.bfloat16(0)) for q in range(LAGS // BP)], axis=0)
        lagged = jnp.dot(table, block_ref[o], preferred_element_type=jnp.float32)
        sums = [zero] * (wide + 1)
        for high in range(LAGS // 8):
            shift = 8 * high
            parts = [lagged[shift:shift + 8, j * LANES:(j + 1) * LANES] for j in range(wide)]
            if shift == 0:
                moved = parts + [None]
            else:
                parts = [pltpu.roll(part, shift, 1) for part in parts]
                keep = lane >= shift
                moved = shifted_in(parts, keep) + [jnp.where(keep, 0.0, parts[-1])]
            sums = [a if b is None else a + b for a, b in zip(sums, moved)]
        sums = [pltpu.roll(part, 0, 1, stride=1, stride_axis=0) for part in sums]
        sums = shifted_in(sums, lane >= row8)
        own = row8 == lax.rem(o, ROWS)
        return tuple(
            jnp.where(own, jnp.sum(part, axis=0, keepdims=True), kept) for part, kept in zip(sums, carry))

    def main_copy(c, d):
        return pltpu.make_async_remote_copy(
            src_ref=main_out.at[c],
            dst_ref=main_in.at[c, d - 1],
            send_sem=main_send.at[c, d - 1], recv_sem=main_recv.at[c, d - 1],
            device_id={"panel": lax.rem(panel + d, panels)}, device_id_type=MESH)

    def tail_copy(c, d):
        return pltpu.make_async_remote_copy(
            src_ref=tail_out.at[c],
            dst_ref=tail_in.at[c, d],
            send_sem=tail_send.at[c, d], recv_sem=tail_recv.at[c, d],
            device_id={"panel": lax.rem(panel + d, panels), "slab": slab + 1}, device_id_type=MESH)

    for c in range(chunks):
        gathered = lax.fori_loop(
            c * ROWS, (c + 1) * ROWS, observer_step, (zero,) * (wide + 1), unroll=UNROLL)
        for j in range(wide):
            lanes = slice(j * LANES, (j + 1) * LANES)
            part_ref[c * ROWS:(c + 1) * ROWS, lanes] = gathered[j]
            main_out[c, :, lanes] = gathered[j].astype(jnp.bfloat16)
        tail_out[c] = gathered[wide].astype(jnp.bfloat16)
        if c == 0:
            pl.semaphore_wait(barrier, panels - 1 + panels * (has_next.astype(jnp.int32) + has_prev.astype(jnp.int32)))

        for d in range(1, panels):
            main_copy(c, d).start()

        @pl.when(has_next)
        def _():
            for d in range(panels):
                tail_copy(c, d).start()

    for c in range(chunks):
        rows = slice(c * ROWS, (c + 1) * ROWS)
        total = part_ref[rows, :]
        for d in range(1, panels):
            main_copy(c, d).wait_recv()
            total = total + main_in[c, d - 1].astype(jnp.float32)
        out_ref[rows, :] = total

        @pl.when(has_prev)
        def _():
            late = None
            for d in range(panels):
                tail_copy(c, d).wait_recv()
                term = tail_in[c, d].astype(jnp.float32)
                late = term if late is None else late + term
            out_ref[rows, :LAGS] += late

    for c in range(chunks):
        for d in range(1, panels):
            main_copy(c, d).wait_send()

        @pl.when(has_next)
        def _():
            for d in range(panels):
                tail_copy(c, d).wait_send()


def shards(panels, slabs, loading, green, delays, offsets, live_groups):
    n_panels, samples = loading.shape
    observers = green.shape[0]
    blocks = delays.shape[1]
    chunks = observers // ROWS
    peers = max(panels - 1, 1)
    anywhere = pl.BlockSpec(memory_space=pl.ANY)
    return pl.pallas_call(
        functools.partial(kernel, panels, slabs),
        out_shape=jax.ShapeDtypeStruct((observers, samples), jnp.float32),
        in_specs=[pl.BlockSpec(memory_space=pltpu.SMEM)] + [anywhere] * 4,
        out_specs=pl.BlockSpec(memory_space=pltpu.VMEM),
        scratch_shapes=[
            pltpu.VMEM((n_panels, samples), jnp.bfloat16),
            pltpu.VMEM((observers, n_panels), jnp.bfloat16),
            pltpu.VMEM((observers, n_panels), jnp.float32),
            pltpu.VMEM((observers, blocks), jnp.int32),
            pltpu.VMEM((observers, blocks), jnp.int32),
            pltpu.VMEM((TAPS, observers, blocks), jnp.float32),
            pltpu.VMEM((observers, blocks, samples), jnp.bfloat16),
            pltpu.VMEM((observers, samples), jnp.float32),
            pltpu.VMEM((chunks, ROWS, samples), jnp.bfloat16),
            pltpu.VMEM((chunks, ROWS, LAGS), jnp.bfloat16),
            pltpu.VMEM((chunks, peers, ROWS, samples), jnp.bfloat16),
            pltpu.VMEM((chunks, panels, ROWS, LAGS), jnp.bfloat16),
            pltpu.SemaphoreType.DMA((LOAD_CHUNKS,)),
            pltpu.SemaphoreType.DMA((LOAD_CHUNKS,)),
            pltpu.SemaphoreType.DMA((2,)),
            pltpu.SemaphoreType.DMA((chunks, peers)),
            pltpu.SemaphoreType.DMA((chunks, peers)),
            pltpu.SemaphoreType.DMA((chunks, panels)),
            pltpu.SemaphoreType.DMA((chunks, panels)),
        ],
        compiler_params=pltpu.CompilerParams(
            collective_id=0, has_side_effects=True, vmem_limit_bytes=56 * 2 ** 20),
        name="far_field",
    )(live_groups, loading, green, delays, offsets)


def solution(mesh):
    placed = (
        P(("case", "panel"), "slab"),
        P(("case", "obs"), "panel"),
        P(("case", "obs"), "panel"),
        P(("case", "obs"), "panel"),
        P("case"),
    )
    return jax.shard_map(
        functools.partial(shards, mesh.shape["panel"], mesh.shape["slab"]),
        mesh=mesh, in_specs=placed, out_specs=P(("case", "obs"), "slab"), check_vma=False,
    )
```

```python
import functools
import math

import jax
import jax.numpy as jnp
from jax import lax
from jax.experimental import pallas as pl
from jax.experimental.pallas import tpu as pltpu
from jax.sharding import PartitionSpec as P

BP = 16
GB = 128
LAGS = 128
TAPS = 8
KT = 256
LANES = 128
ROWS = 8
SHARES = (2, 6, 8, 16)
UNROLL = 8
TILE_UNROLL = 4
MESH = pl.DeviceIdType.MESH


def kernel(panels, slabs, live_hbm, load_hbm, green_hbm, delay_hbm, offset_hbm, out_ref,
           live_ref, load_ref, green_in, green_f32, delay_ref, offset_ref, weight_ref, block_ref, part_ref,
           main_out, tail_out, main_in, tail_in, load_sem, green_sem, small_sem, main_send, main_recv, tail_send, tail_recv):
    panel = lax.axis_index("panel")
    slab = lax.axis_index("slab")
    n_panels, samples = load_hbm.shape
    observers = green_hbm.shape[0]
    blocks = delay_hbm.shape[1]
    chunks = observers // ROWS
    tiles = n_panels // KT
    edges = [tiles * sum(SHARES[:c]) // sum(SHARES) for c in range(len(SHARES) + 1)]
    has_next = slab < slabs - 1
    has_prev = slab > 0

    smalls = [pltpu.make_async_copy(src, dst, small_sem.at[i]) for i, (src, dst) in enumerate(
        ((delay_hbm, delay_ref), (offset_hbm, offset_ref), (live_hbm, live_ref)))]
    loads, greens = [], []
    for c in range(len(SHARES)):
        rows = pl.ds(edges[c] * KT, (edges[c + 1] - edges[c]) * KT)
        greens.append(pltpu.make_async_copy(green_hbm.at[:, rows], green_in.at[:, rows], green_sem.at[c]))
        greens[-1].start()
        loads.append(pltpu.make_async_copy(load_hbm.at[rows, :], load_ref.at[rows, :], load_sem.at[c]))
        loads[-1].start()
    for copy in smalls:
        copy.start()

    barrier = pltpu.get_barrier_semaphore()
    for d in range(1, panels):
        pl.semaphore_signal(barrier, inc=1, device_id={"panel": lax.rem(panel + d, panels)}, device_id_type=MESH)

    @pl.when(has_next)
    def _():
        for d in range(panels):
            pl.semaphore_signal(barrier, inc=1, device_id={
                "panel": lax.rem(panel + d, panels), "slab": slab + 1}, device_id_type=MESH)

    @pl.when(has_prev)
    def _():
        for d in range(panels):
            pl.semaphore_signal(barrier, inc=1, device_id={
                "panel": lax.rem(panel + d, panels), "slab": slab - 1}, device_id_type=MESH)

    block_row = lax.broadcasted_iota(jnp.int32, (BP, KT), 0)
    panel_col = lax.broadcasted_iota(jnp.int32, (BP, KT), 1)
    diagonal = jnp.where(panel_col // BP == block_row, 1.0, 0.0).astype(jnp.bfloat16)

    def tile_step(tile, carry):
        columns = pl.ds(pl.multiple_of(tile * KT, KT), KT)
        pieces = []
        for o in range(observers):
            row = jnp.broadcast_to(green_f32[o:o + 1, columns], (BP, KT)).astype(jnp.bfloat16)
            pieces.append(row * diagonal)
        spread = jnp.concatenate(pieces, axis=0)
        product = jnp.dot(spread, load_ref[columns, :], preferred_element_type=jnp.float32)
        block_ref[:, pl.ds(pl.multiple_of(tile * BP, BP), BP), :] = (
            product.astype(jnp.bfloat16).reshape(observers, BP, samples))
        return carry

    for c in range(len(SHARES)):
        greens[c].wait()
        columns = slice(edges[c] * KT, edges[c + 1] * KT)
        green_f32[:, columns] = green_in[:, columns].astype(jnp.float32)
        loads[c].wait()
        lax.fori_loop(edges[c], edges[c + 1], tile_step, 0, unroll=True)

    for copy in smalls:
        copy.wait()
    position = 3.0 + offset_ref[...].astype(jnp.float32) * 0.125
    terms = [position - float(m) for m in range(TAPS)]
    before = [None] * TAPS
    after = [None] * TAPS
    for k in range(1, TAPS):
        before[k] = terms[k - 1] if k == 1 else before[k - 1] * terms[k - 1]
    for k in range(TAPS - 2, -1, -1):
        after[k] = terms[k + 1] if k == TAPS - 2 else after[k + 1] * terms[k + 1]
    for k in range(TAPS):
        scale = 1.0 / math.prod(k - m for m in range(TAPS) if m != k)
        if k == 0:
            value = after[k]
        elif k == TAPS - 1:
            value = before[k]
        else:
            value = before[k] * after[k]
        weight_ref[k] = value * scale
    live = live_ref[panel]
    group_of = lax.broadcasted_iota(jnp.int32, (observers, blocks), 1) // GB
    delay_ref[...] = jnp.where(group_of < live, delay_ref[...], 4 * LAGS)

    sub = lax.broadcasted_iota(jnp.int32, (BP, blocks), 0)
    lane = lax.broadcasted_iota(jnp.int32, (8, LANES), 1)
    row8 = lax.broadcasted_iota(jnp.int32, (8, LANES), 0)
    wide = samples // LANES
    zero = jnp.zeros((8, LANES), jnp.float32)

    def shifted_in(parts, keep):
        return [jnp.where(keep, parts[0], 0.0)] + [
            jnp.where(keep, parts[j], parts[j - 1]) for j in range(1, len(parts))]

    def observer_step(o, carry):
        behind = sub - delay_ref[pl.ds(o, 1), :]
        tap = behind & (BP - 1)
        place = ((BP - 1 - behind) >> 4).astype(jnp.float32).astype(jnp.bfloat16)
        stencil = jnp.zeros((BP, blocks), jnp.float32)
        for k in range(TAPS):
            stencil = jnp.where(tap == k, weight_ref[k, pl.ds(o, 1), :], stencil)
        stencil = stencil.astype(jnp.bfloat16)
        table = jnp.concatenate([
            jnp.where(place == jnp.bfloat16(q), stencil, jnp.bfloat16(0)) for q in range(LAGS // BP)], axis=0)
        lagged = jnp.dot(table, block_ref[o], preferred_element_type=jnp.float32)
        sums = [zero] * (wide + 1)
        for high in range(LAGS // 8):
            shift = 8 * high
            parts = [lagged[shift:shift + 8, j * LANES:(j + 1) * LANES] for j in range(wide)]
            if shift == 0:
                moved = parts + [None]
            else:
                parts = [pltpu.roll(part, shift, 1) for part in parts]
                keep = lane >= shift
                moved = shifted_in(parts, keep) + [jnp.where(keep, 0.0, parts[-1])]
            sums = [a if b is None else a + b for a, b in zip(sums, moved)]
        sums = [pltpu.roll(part, 0, 1, stride=1, stride_axis=0) for part in sums]
        sums = shifted_in(sums, lane >= row8)
        own = row8 == lax.rem(o, ROWS)
        return tuple(
            jnp.where(own, jnp.sum(part, axis=0, keepdims=True), kept) for part, kept in zip(sums, carry))

    def main_copy(c, d):
        return pltpu.make_async_remote_copy(
            src_ref=main_out.at[c],
            dst_ref=main_in.at[c, d - 1],
            send_sem=main_send.at[c, d - 1], recv_sem=main_recv.at[c, d - 1],
            device_id={"panel": lax.rem(panel + d, panels)}, device_id_type=MESH)

    def tail_copy(c, d):
        return pltpu.make_async_remote_copy(
            src_ref=tail_out.at[c],
            dst_ref=tail_in.at[c, d],
            send_sem=tail_send.at[c, d], recv_sem=tail_recv.at[c, d],
            device_id={"panel": lax.rem(panel + d, panels), "slab": slab + 1}, device_id_type=MESH)

    for c in range(chunks):
        gathered = lax.fori_loop(
            c * ROWS, (c + 1) * ROWS, observer_step, (zero,) * (wide + 1), unroll=UNROLL)
        for j in range(wide):
            lanes = slice(j * LANES, (j + 1) * LANES)
            part_ref[c * ROWS:(c + 1) * ROWS, lanes] = gathered[j]
            main_out[c, :, lanes] = gathered[j].astype(jnp.bfloat16)
        tail_out[c] = gathered[wide].astype(jnp.bfloat16)
        if c == 0:
            pl.semaphore_wait(barrier, panels - 1 + panels * (has_next.astype(jnp.int32) + has_prev.astype(jnp.int32)))

        for d in range(1, panels):
            main_copy(c, d).start()

        @pl.when(has_next)
        def _():
            for d in range(panels):
                tail_copy(c, d).start()

    for c in range(chunks):
        rows = slice(c * ROWS, (c + 1) * ROWS)
        total = part_ref[rows, :]
        for d in range(1, panels):
            main_copy(c, d).wait_recv()
            total = total + main_in[c, d - 1].astype(jnp.float32)
        out_ref[rows, :] = total

        @pl.when(has_prev)
        def _():
            late = None
            for d in range(panels):
                tail_copy(c, d).wait_recv()
                term = tail_in[c, d].astype(jnp.float32)
                late = term if late is None else late + term
            out_ref[rows, :LAGS] += late

    for c in range(chunks):
        for d in range(1, panels):
            main_copy(c, d).wait_send()

        @pl.when(has_next)
        def _():
            for d in range(panels):
                tail_copy(c, d).wait_send()


def shards(panels, slabs, loading, green, delays, offsets, live_groups):
    n_panels, samples = loading.shape
    observers = green.shape[0]
    blocks = delays.shape[1]
    chunks = observers // ROWS
    peers = max(panels - 1, 1)
    anywhere = pl.BlockSpec(memory_space=pltpu.HBM)
    return pl.pallas_call(
        functools.partial(kernel, panels, slabs),
        out_shape=jax.ShapeDtypeStruct((observers, samples), jnp.float32),
        in_specs=[anywhere] * 5,
        out_specs=pl.BlockSpec(memory_space=pltpu.VMEM),
        scratch_shapes=[
            pltpu.SMEM((panels,), jnp.int32),
            pltpu.VMEM((n_panels, samples), jnp.bfloat16),
            pltpu.VMEM((observers, n_panels), jnp.bfloat16),
            pltpu.VMEM((observers, n_panels), jnp.float32),
            pltpu.VMEM((observers, blocks), jnp.int32),
            pltpu.VMEM((observers, blocks), jnp.int32),
            pltpu.VMEM((TAPS, observers, blocks), jnp.float32),
            pltpu.VMEM((observers, blocks, samples), jnp.bfloat16),
            pltpu.VMEM((observers, samples), jnp.float32),
            pltpu.VMEM((chunks, ROWS, samples), jnp.bfloat16),
            pltpu.VMEM((chunks, ROWS, LAGS), jnp.bfloat16),
            pltpu.VMEM((chunks, peers, ROWS, samples), jnp.bfloat16),
            pltpu.VMEM((chunks, panels, ROWS, LAGS), jnp.bfloat16),
            pltpu.SemaphoreType.DMA((len(SHARES),)),
            pltpu.SemaphoreType.DMA((len(SHARES),)),
            pltpu.SemaphoreType.DMA((3,)),
            pltpu.SemaphoreType.DMA((chunks, peers)),
            pltpu.SemaphoreType.DMA((chunks, peers)),
            pltpu.SemaphoreType.DMA((chunks, panels)),
            pltpu.SemaphoreType.DMA((chunks, panels)),
        ],
        compiler_params=pltpu.CompilerParams(
            collective_id=0, has_side_effects=True, vmem_limit_bytes=24 * 2 ** 20),
        name="far_field",
    )(*(pltpu.with_memory_space_constraint(x, pltpu.HBM) for x in (live_groups, loading, green, delays, offsets)))


def solution(mesh):
    placed = (
        P(("case", "panel"), "slab"),
        P(("case", "obs"), "panel"),
        P(("case", "obs"), "panel"),
        P(("case", "obs"), "panel"),
        P("case"),
    )
    return jax.shard_map(
        functools.partial(shards, mesh.shape["panel"], mesh.shape["slab"]),
        mesh=mesh, in_specs=placed, out_specs=P(("case", "obs"), "slab"), check_vma=False,
    )
```

```python
import functools
import math

import jax
import jax.numpy as jnp
from jax import lax
from jax.experimental import pallas as pl
from jax.experimental.pallas import tpu as pltpu
from jax.sharding import PartitionSpec as P

BP = 16
GB = 128
LAGS = 128
TAPS = 8
KT = 256
LANES = 128
ROWS = 8
SHARES = (2, 6, 8, 16)
UNROLL = 8
MESH = pl.DeviceIdType.MESH


def kernel(panels, slabs, live_hbm, load_hbm, green_hbm, delay_hbm, offset_hbm, out_ref,
           live_ref, load_ref, green_in, delay_ref, offset_ref, weight_ref, block_ref, part_ref,
           main_out, tail_out, main_in, tail_in, load_sem, green_sem, small_sem, main_send, main_recv, tail_send, tail_recv):
    panel = lax.axis_index("panel")
    slab = lax.axis_index("slab")
    n_panels, samples = load_hbm.shape
    observers = green_hbm.shape[0]
    blocks = delay_hbm.shape[1]
    chunks = observers // ROWS
    tiles = n_panels // KT
    edges = [tiles * sum(SHARES[:c]) // sum(SHARES) for c in range(len(SHARES) + 1)]
    has_next = slab < slabs - 1
    has_prev = slab > 0

    smalls = [pltpu.make_async_copy(src, dst, small_sem.at[i]) for i, (src, dst) in enumerate(
        ((delay_hbm, delay_ref), (offset_hbm, offset_ref), (live_hbm, live_ref)))]
    loads, greens = [], []
    for c in range(len(SHARES)):
        rows = pl.ds(edges[c] * KT, (edges[c + 1] - edges[c]) * KT)
        greens.append(pltpu.make_async_copy(green_hbm.at[:, rows], green_in.at[:, rows], green_sem.at[c]))
        greens[-1].start()
        loads.append(pltpu.make_async_copy(load_hbm.at[rows, :], load_ref.at[rows, :], load_sem.at[c]))
        loads[-1].start()
    for copy in smalls:
        copy.start()

    barrier = pltpu.get_barrier_semaphore()
    for d in range(1, panels):
        pl.semaphore_signal(barrier, inc=1, device_id={"panel": lax.rem(panel + d, panels)}, device_id_type=MESH)

    @pl.when(has_next)
    def _():
        for d in range(panels):
            pl.semaphore_signal(barrier, inc=1, device_id={
                "panel": lax.rem(panel + d, panels), "slab": slab + 1}, device_id_type=MESH)

    @pl.when(has_prev)
    def _():
        for d in range(panels):
            pl.semaphore_signal(barrier, inc=1, device_id={
                "panel": lax.rem(panel + d, panels), "slab": slab - 1}, device_id_type=MESH)

    block_row = lax.broadcasted_iota(jnp.int32, (BP, KT), 0)
    panel_col = lax.broadcasted_iota(jnp.int32, (BP, KT), 1)
    diagonal = jnp.where(panel_col // BP == block_row, 1.0, 0.0).astype(jnp.bfloat16)

    def tile_step(tile, carry):
        columns = pl.ds(pl.multiple_of(tile * KT, KT), KT)
        pieces = []
        for o in range(observers):
            row = jnp.broadcast_to(green_in[o:o + 1, columns], (BP, KT))
            pieces.append(row * diagonal)
        spread = jnp.concatenate(pieces, axis=0)
        product = jnp.dot(spread, load_ref[columns, :], preferred_element_type=jnp.float32)
        block_ref[:, pl.ds(pl.multiple_of(tile * BP, BP), BP), :] = (
            product.astype(jnp.bfloat16).reshape(observers, BP, samples))
        return carry

    for c in range(len(SHARES)):
        greens[c].wait()
        loads[c].wait()
        lax.fori_loop(edges[c], edges[c + 1], tile_step, 0, unroll=True)

    for copy in smalls:
        copy.wait()
    position = 3.0 + offset_ref[...].astype(jnp.float32) * 0.125
    terms = [position - float(m) for m in range(TAPS)]
    before = [None] * TAPS
    after = [None] * TAPS
    for k in range(1, TAPS):
        before[k] = terms[k - 1] if k == 1 else before[k - 1] * terms[k - 1]
    for k in range(TAPS - 2, -1, -1):
        after[k] = terms[k + 1] if k == TAPS - 2 else after[k + 1] * terms[k + 1]
    for k in range(TAPS):
        scale = 1.0 / math.prod(k - m for m in range(TAPS) if m != k)
        if k == 0:
            value = after[k]
        elif k == TAPS - 1:
            value = before[k]
        else:
            value = before[k] * after[k]
        weight_ref[k] = value * scale
    live = live_ref[panel]
    group_of = lax.broadcasted_iota(jnp.int32, (observers, blocks), 1) // GB
    delay_ref[...] = jnp.where(group_of < live, delay_ref[...], 4 * LAGS)

    sub = lax.broadcasted_iota(jnp.int32, (BP, blocks), 0)
    lane = lax.broadcasted_iota(jnp.int32, (8, LANES), 1)
    row8 = lax.broadcasted_iota(jnp.int32, (8, LANES), 0)
    wide = samples // LANES
    zero = jnp.zeros((8, LANES), jnp.float32)

    def shifted_in(parts, keep):
        return [jnp.where(keep, parts[0], 0.0)] + [
            jnp.where(keep, parts[j], parts[j - 1]) for j in range(1, len(parts))]

    def observer_step(o, carry):
        behind = sub - delay_ref[pl.ds(o, 1), :]
        tap = behind & (BP - 1)
        place = ((BP - 1 - behind) >> 4).astype(jnp.float32).astype(jnp.bfloat16)
        stencil = jnp.zeros((BP, blocks), jnp.float32)
        for k in range(TAPS):
            stencil = jnp.where(tap == k, weight_ref[k, pl.ds(o, 1), :], stencil)
        stencil = stencil.astype(jnp.bfloat16)
        table = jnp.concatenate([
            jnp.where(place == jnp.bfloat16(q), stencil, jnp.bfloat16(0)) for q in range(LAGS // BP)], axis=0)
        lagged = jnp.dot(table, block_ref[o], preferred_element_type=jnp.float32)
        sums = [zero] * (wide + 1)
        for high in range(LAGS // 8):
            shift = 8 * high
            parts = [lagged[shift:shift + 8, j * LANES:(j + 1) * LANES] for j in range(wide)]
            if shift == 0:
                moved = parts + [None]
            else:
                parts = [pltpu.roll(part, shift, 1) for part in parts]
                keep = lane >= shift
                moved = shifted_in(parts, keep) + [jnp.where(keep, 0.0, parts[-1])]
            sums = [a if b is None else a + b for a, b in zip(sums, moved)]
        sums = [pltpu.roll(part, 0, 1, stride=1, stride_axis=0) for part in sums]
        sums = shifted_in(sums, lane >= row8)
        own = row8 == lax.rem(o, ROWS)
        return tuple(
            jnp.where(own, jnp.sum(part, axis=0, keepdims=True), kept) for part, kept in zip(sums, carry))

    def main_copy(c, d):
        return pltpu.make_async_remote_copy(
            src_ref=main_out.at[c],
            dst_ref=main_in.at[c, d - 1],
            send_sem=main_send.at[c, d - 1], recv_sem=main_recv.at[c, d - 1],
            device_id={"panel": lax.rem(panel + d, panels)}, device_id_type=MESH)

    def tail_copy(c, d):
        return pltpu.make_async_remote_copy(
            src_ref=tail_out.at[c],
            dst_ref=tail_in.at[c, d],
            send_sem=tail_send.at[c, d], recv_sem=tail_recv.at[c, d],
            device_id={"panel": lax.rem(panel + d, panels), "slab": slab + 1}, device_id_type=MESH)

    for c in range(chunks):
        gathered = lax.fori_loop(
            c * ROWS, (c + 1) * ROWS, observer_step, (zero,) * (wide + 1), unroll=UNROLL)
        for j in range(wide):
            lanes = slice(j * LANES, (j + 1) * LANES)
            part_ref[c * ROWS:(c + 1) * ROWS, lanes] = gathered[j]
            main_out[c, :, lanes] = gathered[j].astype(jnp.bfloat16)
        tail_out[c] = gathered[wide].astype(jnp.bfloat16)
        if c == 0:
            pl.semaphore_wait(barrier, panels - 1 + panels * (has_next.astype(jnp.int32) + has_prev.astype(jnp.int32)))

        for d in range(1, panels):
            main_copy(c, d).start()

        @pl.when(has_next)
        def _():
            for d in range(panels):
                tail_copy(c, d).start()

    for c in range(chunks):
        rows = slice(c * ROWS, (c + 1) * ROWS)
        total = part_ref[rows, :]
        for d in range(1, panels):
            main_copy(c, d).wait_recv()
            total = total + main_in[c, d - 1].astype(jnp.float32)
        out_ref[rows, :] = total

        @pl.when(has_prev)
        def _():
            late = None
            for d in range(panels):
                tail_copy(c, d).wait_recv()
                term = tail_in[c, d].astype(jnp.float32)
                late = term if late is None else late + term
            out_ref[rows, :LAGS] += late

    for c in range(chunks):
        for d in range(1, panels):
            main_copy(c, d).wait_send()

        @pl.when(has_next)
        def _():
            for d in range(panels):
                tail_copy(c, d).wait_send()


def shards(panels, slabs, loading, green, delays, offsets, live_groups):
    n_panels, samples = loading.shape
    observers = green.shape[0]
    blocks = delays.shape[1]
    chunks = observers // ROWS
    peers = max(panels - 1, 1)
    anywhere = pl.BlockSpec(memory_space=pltpu.HBM)
    return pl.pallas_call(
        functools.partial(kernel, panels, slabs),
        out_shape=jax.ShapeDtypeStruct((observers, samples), jnp.float32),
        in_specs=[anywhere] * 5,
        out_specs=pl.BlockSpec(memory_space=pltpu.VMEM),
        scratch_shapes=[
            pltpu.SMEM((panels,), jnp.int32),
            pltpu.VMEM((n_panels, samples), jnp.bfloat16),
            pltpu.VMEM((observers, n_panels), jnp.bfloat16),
            pltpu.VMEM((observers, blocks), jnp.int32),
            pltpu.VMEM((observers, blocks), jnp.int32),
            pltpu.VMEM((TAPS, observers, blocks), jnp.float32),
            pltpu.VMEM((observers, blocks, samples), jnp.bfloat16),
            pltpu.VMEM((observers, samples), jnp.float32),
            pltpu.VMEM((chunks, ROWS, samples), jnp.bfloat16),
            pltpu.VMEM((chunks, ROWS, LAGS), jnp.bfloat16),
            pltpu.VMEM((chunks, peers, ROWS, samples), jnp.bfloat16),
            pltpu.VMEM((chunks, panels, ROWS, LAGS), jnp.bfloat16),
            pltpu.SemaphoreType.DMA((len(SHARES),)),
            pltpu.SemaphoreType.DMA((len(SHARES),)),
            pltpu.SemaphoreType.DMA((3,)),
            pltpu.SemaphoreType.DMA((chunks, peers)),
            pltpu.SemaphoreType.DMA((chunks, peers)),
            pltpu.SemaphoreType.DMA((chunks, panels)),
            pltpu.SemaphoreType.DMA((chunks, panels)),
        ],
        compiler_params=pltpu.CompilerParams(
            collective_id=0, has_side_effects=True, vmem_limit_bytes=24 * 2 ** 20),
        name="far_field",
    )(*(pltpu.with_memory_space_constraint(x, pltpu.HBM) for x in (live_groups, loading, green, delays, offsets)))


def solution(mesh):
    placed = (
        P(("case", "panel"), "slab"),
        P(("case", "obs"), "panel"),
        P(("case", "obs"), "panel"),
        P(("case", "obs"), "panel"),
        P("case"),
    )
    return jax.shard_map(
        functools.partial(shards, mesh.shape["panel"], mesh.shape["slab"]),
        mesh=mesh, in_specs=placed, out_specs=P(("case", "obs"), "slab"), check_vma=False,
    )
```
